512 devices in a mesh: dp: 4 (over x_lo, core), expert: 128 (over y, x_hi, z).
Axes of the slice: x: 4 (x_hi: 2, x_lo: 2; x = x_hi * 2 + x_lo), y: 4, z: 16, core: 2. Of those that a mesh axis runs over, the one named last changes fastest.
Arguments:
- activations: bfloat16 [65536, 2048], P(('dp', 'expert')), may hold values from -6 to 6
- routed_experts: int32 [65536, 2], P(('dp', 'expert')), may hold values from 0 to 127, all different within a row; in each aligned block of 128 rows (0 to 127, 128 to 255, ...) at most 2 rows name the same one
- route_weights: float32 [65536, 2], P(('dp', 'expert')), may hold values from 0.25 to 1
- live_counts: int32 [4, 128], P('dp', 'expert'), may hold values from 32 to 128, as said below
- swap_partner: int32 [128], replicated, may hold values from 0 to 127, as said below
- gate_proj: bfloat16 [128, 2048, 768], P('expert', 'dp'), may hold values from -0.125 to 0.125
- up_proj: bfloat16 [128, 2048, 768], P('expert', 'dp'), may hold values from -0.125 to 0.125
- down_proj: bfloat16 [128, 2048, 768], P('expert', 'dp'), may hold values from -0.21875 to 0.21875
- first_moment: bfloat16 [128, 2048, 768], P('expert', 'dp'), may hold values from -6 to 6
- second_moment: bfloat16 [128, 2048], P('expert', 'dp'), may hold values from 0.5 to 20
Outputs:
- layer_output: bfloat16 [65536, 2048], P(('dp', 'expert'))
- update_direction: bfloat16 [128, 2048, 768], P('expert', 'dp')
The draws below stay inside these ranges and needn't reach their ends.
Inputs may be any that keep to these rules, and one draw needn't show every extreme that they name: `routed_experts`: each token names 2 different experts; the 256 routed rows of one device name every expert exactly 2 times. The first live_counts tokens of a device's block are live, the rest are padding; some device has all 128 live. swap_partner[i] = i XOR p, where p is 64 or 32, the same for all i, so devices are swapped in pairs; expert i moves to device swap_partner[i].
All inputs are finite; a program needn't handle non-finite values.
Results may differ from the reference program's by a relative error of at most 0.015.
Values may be sent and summed in bfloat16 or wider, within the bound.
A program may use at most 64 MiB of HBM per device.

```python
import math
import jax
import jax.numpy as jnp
import numpy as np
from jax import lax

D = 2048
FW = 768
TOPF = 2
TOK_DEV = 128
EXPERTS = 128
CAP = 2
TOKENS = 65536
N_DP = 4
N_EXPERT = 128


def draw_swap_partner(key, part):
    levels = EXPERTS.bit_length() - 1
    bit_place = jax.random.randint(key, (), levels - 2, levels)
    power = jnp.left_shift(jnp.int32(1), bit_place.astype(jnp.int32))
    return jnp.bitwise_xor(jnp.arange(EXPERTS, dtype=jnp.int32), power).astype(jnp.int32)


def draw_live_counts(key, part):
    lowest = max(TOK_DEV // 4, 1)
    drawn = jax.random.randint(key, (N_DP * N_EXPERT,), lowest, TOK_DEV + 1)
    chosen = jax.random.randint(jax.random.fold_in(key, 7), (), 0, N_DP * N_EXPERT)
    flattened = jnp.where(jnp.arange(N_DP * N_EXPERT) == chosen, TOK_DEV, drawn)
    return flattened.reshape(N_DP, N_EXPERT).astype(jnp.int32)


def block_levels(key, extent, split, least, high):
    gain, own = 1.0, jax.random.fold_in(key, 6)
    for dim, shards_of in split:
        heights = jnp.exp(jax.random.uniform(jax.random.fold_in(own, dim), (shards_of,), jnp.float32, least / len(split), high / len(split)))
        gain = gain * jnp.repeat(heights, extent[dim] // shards_of).reshape([-1 if axis == dim else 1 for axis in range(len(extent))])
    return gain


def shared_out(stream_key, own, number, rows, amount, top, limit, skew):
    ranking = jax.random.permutation(stream_key, amount)
    heavy_load, ordinary = shares(amount, rows * top, limit, skew, True), shares(amount, rows * top, limit, skew, False)
    places = jnp.arange(amount)

    def named(sizes, turn):
        used = int((sizes > 0).sum())
        fixed = max(1, used // 4)
        shifted = fixed + (places - fixed + turn * (used - fixed)) % max(1, amount - fixed)
        return jnp.zeros((amount,), jnp.int32).at[ranking[jnp.where(places < fixed, places, shifted)]].set(jnp.asarray(sizes, jnp.int32))

    sizes = jnp.where(number % 4 == 0, named(heavy_load, number // 4), named(ordinary, number - number // 4 - 1))
    mixed = jax.random.permutation(jax.random.fold_in(own, 3), amount)
    donor, taker = mixed[0:amount // 2 * 2:2], mixed[1:amount // 2 * 2:2]
    slack = jnp.minimum(sizes[donor] - 1, limit - sizes[taker]) // 2
    slack = jnp.where((donor == ranking[0]) | (taker == ranking[0]) | (sizes[taker] == 0), 0, jnp.maximum(slack, 0))
    shifted = jax.random.randint(jax.random.fold_in(own, 4), (amount // 2,), 0, 1 << 20) % (slack + 1)
    sizes = sizes.at[donor].add(-shifted).at[taker].add(shifted)
    members = jnp.searchsorted(jnp.cumsum(sizes), jnp.arange(rows * top), side="right").astype(jnp.int32)
    table = members.reshape(top, rows).T
    table = table[jax.random.permutation(jax.random.fold_in(own, 1), rows)]
    turn = jax.random.randint(jax.random.fold_in(own, 2), (rows, 1), 0, top)
    return jnp.take_along_axis(table, (jnp.arange(top)[None, :] + turn) % top, axis=1)


def shares(number_of, total, most, slope, full):
    weights = [(1 << 20) // math.isqrt(standing ** slope) + 1 for standing in range(1, number_of + 1)]
    largest = most if full else min(most, max(-(-total // number_of), total * weights[0] // sum(weights)))
    least = 1 if total - largest >= number_of - 1 else 0
    counts, rest = [largest] + [least] * (number_of - 1), total - largest - least * (number_of - 1)
    while rest > 0:
        movable = [i for i in range(1, number_of) if counts[i] < largest] or [i for i in range(1, number_of) if counts[i] < most]
        mass, budget = sum([weights[i] for i in movable]), rest
        for i in movable:
            more = min(most - counts[i], max(1, budget * weights[i] // mass), rest)
            counts[i] = counts[i] + more
            rest = rest - more
    return np.array(counts)


def bell_draw(rng, extent, width, bound, split=(), held_as=jnp.bfloat16):
    values = width * jax.random.normal(rng, extent, jnp.float32)
    if split:
        values = values * block_levels(rng, extent, split, -0.22, 0.18)
    return jnp.clip(values, -bound, bound).astype(held_as)


def setup_inputs(seed: int = 0) -> dict:
    arg_keys = jax.random.split(jax.random.key(seed), 11)
    activations = bell_draw(arg_keys[0], (TOKENS, D), 1.0, 6.0, ((0, 512),))
    routed_experts_keys = jax.random.split(jax.random.fold_in(arg_keys[1], 1), TOKENS // TOK_DEV)
    routed_experts_turns = jax.random.permutation(jax.random.fold_in(arg_keys[1], 3), TOKENS // TOK_DEV)
    routed_experts = jax.vmap(lambda own, number: shared_out(jax.random.fold_in(arg_keys[1], 2), own, number, TOK_DEV, EXPERTS, TOPF, CAP, 0))(routed_experts_keys, routed_experts_turns).reshape((TOKENS, TOPF))
    route_weights = jnp.clip(0.25 + 0.75 * jax.random.uniform(arg_keys[2], (TOKENS, TOPF), jnp.float32) ** block_levels(arg_keys[2], (TOKENS, TOPF), ((0, 512),), -0.2, 0.2), 0.25, 1.0)
    live_counts = draw_live_counts(jax.random.fold_in(arg_keys[10], 71), 0)
    swap_partner = draw_swap_partner(jax.random.fold_in(arg_keys[10], 71), 0)
    gate_proj = bell_draw(arg_keys[5], (EXPERTS, D, FW), D ** -0.5, 0.125, ((0, 128), (1, 4)))
    up_proj = bell_draw(arg_keys[6], (EXPERTS, D, FW), D ** -0.5, 0.125, ((0, 128), (1, 4)))
    down_proj = bell_draw(arg_keys[7], (EXPERTS, D, FW), FW ** -0.5, 0.21875, ((0, 128), (1, 4)))
    first_moment = bell_draw(arg_keys[8], (EXPERTS, D, FW), 1.0, 6.0, ((0, 128), (1, 4)))
    second_moment = jnp.clip(jnp.exp(math.log(20.0) - 3.6888795 * jax.random.uniform(arg_keys[9], (EXPERTS, D), jnp.float32) ** block_levels(arg_keys[9], (EXPERTS, D), ((0, 128), (1, 4)), -0.2, 0.2)), 0.5, 20.0).astype(jnp.bfloat16)
    return {"activations": activations, "routed_experts": routed_experts, "route_weights": route_weights, "live_counts": live_counts, "swap_partner": swap_partner, "gate_proj": gate_proj, "up_proj": up_proj, "down_proj": down_proj, "first_moment": first_moment, "second_moment": second_moment}


def reference(activations, routed_experts, route_weights, live_counts, swap_partner, gate_proj, up_proj, down_proj, first_moment, second_moment):
    devices = N_DP * N_EXPERT
    routed = TOK_DEV * TOPF
    expert_ids = routed_experts.reshape(devices, routed)
    columns = jnp.arange(EXPERTS, dtype=jnp.int32)
    matches = (expert_ids[:, :, None] == columns[None, None, :]).astype(jnp.int32)
    rank_table = lax.optimization_barrier(jnp.sum(matches * (jnp.cumsum(matches, axis=1) - 1), axis=2)).astype(jnp.int32)
    device_index = jnp.broadcast_to(jnp.arange(devices, dtype=jnp.int32)[:, None], (devices, routed))
    row_index = jnp.broadcast_to(jnp.arange(routed, dtype=jnp.int32)[None, :], (devices, routed))
    placed = jnp.zeros((EXPERTS, devices, CAP), jnp.int32).at[expert_ids, device_index, rank_table].set(row_index)
    token_rows = activations.reshape(devices, TOK_DEV, D)
    device_column = jnp.arange(devices, dtype=jnp.int32)[:, None]

    def forward_expert(operands):
        placement_rows, gate_w, up_w, down_w = operands
        chosen = token_rows[device_column, placement_rows // TOPF].reshape(devices * CAP, D)
        gate_sum = jnp.dot(chosen, gate_w, preferred_element_type=jnp.float32)
        up_sum = jnp.dot(chosen, up_w, preferred_element_type=jnp.float32)
        hidden = (jax.nn.silu(gate_sum) * up_sum).astype(jnp.bfloat16)
        produced = jnp.dot(hidden, down_w.T, preferred_element_type=jnp.float32).astype(jnp.bfloat16)
        return (produced.reshape(devices, CAP, D), hidden.reshape(devices, CAP, FW))
    produced_all, hidden_all = lax.map(forward_expert, (placed, gate_proj, up_proj, down_proj))
    gathered = produced_all[expert_ids, device_index, rank_table].reshape(devices, TOK_DEV, TOPF, D)
    weights = route_weights.reshape(devices, TOK_DEV, TOPF)
    total = jnp.zeros((devices, TOK_DEV, D), jnp.float32)
    for choice_index in range(TOPF):
        total = total + gathered[:, :, choice_index].astype(jnp.float32) * weights[:, :, choice_index, None]
    live_mask = (jnp.arange(TOK_DEV, dtype=jnp.int32)[None, :] < live_counts.reshape(devices)[:, None]).astype(jnp.float32)
    layer_output = (total * live_mask[:, :, None]).astype(jnp.bfloat16)
    cotangent = (weights[:, :, :, None] * layer_output.astype(jnp.float32)[:, :, None, :]).astype(jnp.bfloat16)
    cotangent = cotangent.reshape(devices, routed, D)

    def update_expert(operands):
        placement_rows, hidden, first_state, second_state = operands
        picked = cotangent[device_column, placement_rows].reshape(N_DP, N_EXPERT * CAP, D).astype(jnp.float32)
        hidden_group = hidden.reshape(N_DP, N_EXPERT * CAP, FW).astype(jnp.float32)
        partial_sums = jnp.einsum('qrd,qrf->qdf', picked, hidden_group).astype(jnp.bfloat16)
        gradient = lax.optimization_barrier(jnp.sum(partial_sums.astype(jnp.float32), axis=0))
        first_new = 0.9 * first_state.astype(jnp.float32) + 0.1 * gradient
        second_new = 0.99 * second_state.astype(jnp.float32) + 0.01 * lax.optimization_barrier(jnp.mean(gradient * gradient, axis=1))
        return (first_new / (jnp.sqrt(second_new)[:, None] + 1e-08)).astype(jnp.bfloat16)
    steps_all = lax.map(update_expert, (placed, hidden_all, first_moment, second_moment))
    update_direction = steps_all[swap_partner]
    return (layer_output.reshape(TOKENS, D), update_direction)
```

```python
import jax
import jax.numpy as jnp
from jax import lax
from jax.sharding import PartitionSpec as P

F32 = jnp.float32
BF16 = jnp.bfloat16


def exchange(block, axis, distance):
    count = lax.axis_size(axis)
    return lax.ppermute(block, axis, [(i, i ^ distance) for i in range(count)])


def dot(a, b):
    return jnp.dot(a, b, preferred_element_type=F32)


def slot_table(ids, experts, capacity):
    tokens = ids.shape[0]
    slot = lax.broadcasted_iota(jnp.int32, (experts * capacity, tokens), 0)
    named = slot // capacity
    match = (named == ids[:, 0][None, :]) | (named == ids[:, 1][None, :])
    earlier = (
        lax.broadcasted_iota(jnp.int32, (tokens, tokens), 0)
        < lax.broadcasted_iota(jnp.int32, (tokens, tokens), 1)
    ).astype(BF16)
    rank = dot(match.astype(BF16), earlier)
    return match & (rank == (slot % capacity).astype(F32)), named


def local(
    activations,
    routed_experts,
    route_weights,
    live_counts,
    swap_partner,
    gate_proj,
    up_proj,
    down_proj,
    first_moment,
    second_moment,
):
    experts = swap_partner.shape[0]
    tokens, choices = routed_experts.shape
    width = activations.shape[1]
    capacity = tokens * choices // experts
    rows = experts * capacity
    part = gate_proj.shape[1]
    groups = lax.axis_size("dp")
    q = lax.axis_index("dp")
    partner = swap_partner[0]
    far, near = experts // 2, experts // 4

    def to_experts(block):
        block = block.reshape(experts, capacity, width)
        out = lax.all_to_all(block, "expert", split_axis=0, concat_axis=0, tiled=True)
        return out.reshape(rows, width)

    def moved(block):
        return jnp.where(
            partner == far, exchange(block, "expert", far), exchange(block, "expert", near)
        )

    def shards(weight):
        own = weight[0]
        across = exchange(own, "dp", 2)
        return own, exchange(own, "dp", 1), across, exchange(across, "dp", 1)

    place, named = slot_table(routed_experts, experts, capacity)
    outgoing = dot(place.astype(BF16), activations).astype(BF16)
    arrived = to_experts(outgoing)
    gates, ups, downs = shards(gate_proj), shards(up_proj), shards(down_proj)
    first_here = moved(first_moment[0])
    second_here = moved(second_moment[0])

    gate_sum = jnp.zeros((rows, gate_proj.shape[2]), F32)
    up_sum = gate_sum
    for m in range(groups):
        columns = lax.dynamic_slice_in_dim(arrived, (q ^ m) * part, part, axis=1)
        gate_sum = gate_sum + dot(columns, gates[m])
        up_sum = up_sum + dot(columns, ups[m])
    hidden = (jax.nn.silu(gate_sum) * up_sum).astype(BF16)
    produced = jnp.stack(
        [
            jnp.einsum("rf,nf->rn", hidden, downs[m], preferred_element_type=F32).astype(BF16)
            for m in range(groups)
        ]
    )
    produced = jnp.concatenate(
        [lax.dynamic_index_in_dim(produced, q ^ b, 0, keepdims=False) for b in range(groups)],
        axis=1,
    )
    returned = to_experts(produced)
    hidden_here = lax.all_gather(moved(hidden), "dp", axis=0, tiled=True)

    total = jnp.zeros((tokens, width), F32)
    for k in range(choices):
        pick = (place & (named == routed_experts[:, k][None, :])).astype(BF16)
        picked = lax.dot_general(
            pick, returned, (((0,), (0,)), ((), ())), preferred_element_type=F32
        )
        total = total + picked * route_weights[:, k, None]
    live = (jnp.arange(tokens, dtype=jnp.int32) < live_counts[0, 0]).astype(F32)
    layer_output = (total * live[:, None]).astype(BF16)

    new_place, new_named = slot_table(routed_experts ^ partner, experts, capacity)
    first_choice = new_named == (routed_experts[:, 0] ^ partner)[None, :]
    slot_weight = jnp.sum(
        jnp.where(
            new_place,
            jnp.where(first_choice, route_weights[:, 0][None, :], route_weights[:, 1][None, :]),
            0.0,
        ),
        axis=1,
        keepdims=True,
    )
    cotangent = (slot_weight * dot(new_place.astype(BF16), layer_output)).astype(BF16)
    cotangent = to_experts(cotangent)
    own_part = lax.all_to_all(cotangent, "dp", split_axis=1, concat_axis=0, tiled=True)
    gradient = lax.dot_general(
        own_part, hidden_here, (((0,), (0,)), ((), ())), preferred_element_type=F32
    )
    first_new = 0.9 * first_here.astype(F32) + 0.1 * gradient
    second_new = 0.99 * second_here.astype(F32) + 0.01 * jnp.mean(gradient * gradient, axis=1)
    update = (first_new / (jnp.sqrt(second_new)[:, None] + 1e-08)).astype(BF16)
    return layer_output, update[None]


def solution(mesh):
    in_specs = (
        P(("dp", "expert"), None),
        P(("dp", "expert"), None),
        P(("dp", "expert"), None),
        P("dp", "expert"),
        P(),
        P("expert", "dp", None),
        P("expert", "dp", None),
        P("expert", "dp", None),
        P("expert", "dp", None),
        P("expert", "dp"),
    )
    out_specs = (P(("dp", "expert"), None), P("expert", "dp", None))
    return jax.shard_map(local, mesh=mesh, in_specs=in_specs, out_specs=out_specs, check_vma=False)
```
